256 devices in a mesh: expert: 16 (over z_hi, x, core), replica: 16 (over z_lo, y).
Axes of the slice: x: 4, y: 4, z: 8 (z_hi: 2, z_lo: 4; z = z_hi * 4 + z_lo), core: 2. Of those that a mesh axis runs over, the one named last changes fastest.
Arguments:
- tokens: bfloat16 [16, 4096, 2048], P('replica', 'expert'), may hold values from -6 to 6
- out_grad: bfloat16 [16, 4096, 2048], P('replica', 'expert'), may hold values from -6 to 6
- routes: int32 [16, 4096, 2], P('replica', 'expert'), may hold values from 0 to 15, all different within a row; in each aligned block of 256 rows (0 to 255, 256 to 511, ..., all dimensions but the last counted through in order) at most 64 rows name the same one
- route_weight: bfloat16 [16, 4096, 2], P('replica', 'expert'), may hold values from 0.19921875 to 1
- gate_up_matrix: bfloat16 [16, 16, 2048, 512], P('replica', 'expert'), may hold values from -6 to 6
- down_matrix: bfloat16 [16, 16, 2048, 256], P('replica', 'expert'), may hold values from -6 to 6
- gate_up_velocity: bfloat16 [16, 16, 2048, 512], P('replica', 'expert'), may hold values from -6 to 6
- down_velocity: bfloat16 [16, 16, 2048, 256], P('replica', 'expert'), may hold values from -6 to 6
- partner: int32 [16], replicated, may hold values from 0 to 15, as said below
Outputs:
- token_grad: bfloat16 [16, 4096, 2048], P('replica', 'expert')
- mixed_gate_up: bfloat16 [16, 16, 2048, 512], P('replica', 'expert')
- mixed_down: bfloat16 [16, 16, 2048, 256], P('replica', 'expert')
The draws below stay inside these ranges and needn't reach their ends.
Inputs may be any that keep to these rules, and one draw needn't show every extreme that they name: `routes`: the rows of one device route at most 64 pairs to any one expert; no row names an expert twice. partner[r] = r xor s for one power of two s below 16, the same s for all r, so replicas are matched in pairs.
All inputs are finite; a program needn't handle non-finite values.
Results may differ from the reference program's by a relative error of at most 0.0065.
Values may be sent and summed in bfloat16 or wider, within the bound.
A program may use at most 128 MiB of HBM per device.

```python
import math
import jax
import jax.numpy as jnp
import numpy as np
from jax import lax

MODEL_WIDTH = 2048
FF = 256
TOP = 2
TOK_DEV = 256
EXPERT_TOTAL = 16
REPLICAS = 16
CAP = 64
ROWS = 4096
N_EXPERT = 16


def draw_partner(key, part):
    levels = REPLICAS.bit_length() - 1
    level = jax.random.randint(jax.random.fold_in(key, 17), (), 0, levels, dtype=jnp.int32)
    offset = jnp.left_shift(jnp.ones((), jnp.int32), level)
    return jnp.bitwise_xor(jnp.arange(REPLICAS, dtype=jnp.int32), offset).astype(jnp.int32)


def block_levels(own_key, extent, cuts, smallest, high):
    def one(axis_at, parts):
        steps = jax.random.uniform(jax.random.fold_in(jax.random.fold_in(own_key, 6), axis_at), (parts,), jnp.float32, smallest / len(cuts), high / len(cuts))
        return jnp.repeat(jnp.exp(steps), extent[axis_at] // parts).reshape((-1,) + (1,) * (len(extent) - axis_at - 1))

    factor_of = one(*cuts[0])
    for cut in cuts[1:]:
        factor_of = factor_of * one(*cut)
    return factor_of


def assign_block(rng, own, number, rows, number_of, top, most, lean):
    order = jax.random.permutation(rng, number_of)
    heavy_load, common = portions_of(number_of, rows * top, most, lean, True), portions_of(number_of, rows * top, most, lean, False)
    places = jnp.arange(number_of)

    def named(sizes, rotation):
        used = int((sizes > 0).sum())
        fixed = max(1, used // 4)
        shifted = fixed + (places - fixed + rotation * (used - fixed)) % max(1, number_of - fixed)
        return jnp.zeros((number_of,), jnp.int32).at[order[jnp.where(places < fixed, places, shifted)]].set(jnp.asarray(sizes, jnp.int32))

    sizes = jnp.where(number % 4 == 0, named(heavy_load, number // 4), named(common, number - number // 4 - 1))
    mixed = jax.random.permutation(jax.random.fold_in(own, 3), number_of)
    giver, taker = mixed[0:number_of // 2 * 2:2], mixed[1:number_of // 2 * 2:2]
    margin = jnp.minimum(sizes[giver] - 1, most - sizes[taker]) // 2
    margin = jnp.where((giver == order[0]) | (taker == order[0]) | (sizes[taker] == 0), 0, jnp.maximum(margin, 0))
    shifted = jax.random.randint(jax.random.fold_in(own, 4), (number_of // 2,), 0, 1 << 20) % (margin + 1)
    sizes = sizes.at[giver].add(-shifted).at[taker].add(shifted)
    items = jnp.searchsorted(jnp.cumsum(sizes), jnp.arange(rows * top), side="right").astype(jnp.int32)
    listing = items.reshape(top, rows).T
    listing = listing[jax.random.permutation(jax.random.fold_in(own, 1), rows)]
    rotation = jax.random.randint(jax.random.fold_in(own, 2), (rows, 1), 0, top)
    return jnp.take_along_axis(listing, (jnp.arange(top)[None, :] + rotation) % top, axis=1)


def portions_of(number_of, total, most, skew, full):
    loads = [(1 << 20) // math.isqrt(grade ** skew) + 1 for grade in range(1, number_of + 1)]
    largest = most if full else min(most, max(-(-total // number_of), total * loads[0] // sum(loads)))
    least = 1 if total - largest >= number_of - 1 else 0
    holding, rest = [largest] + [least] * (number_of - 1), total - largest - least * (number_of - 1)
    while rest > 0:
        candidates = [i for i in range(1, number_of) if holding[i] < largest] or [i for i in range(1, number_of) if holding[i] < most]
        whole, left = sum([loads[i] for i in candidates]), rest
        for i in candidates:
            addition = min(most - holding[i], max(1, left * loads[i] // whole), rest)
            holding[i] = holding[i] + addition
            rest = rest - addition
    return np.array(holding)


def noise(own_key, dims, spread, most, cuts=(), kind=jnp.bfloat16):
    entries = spread * jax.random.normal(own_key, dims, jnp.float32)
    if cuts:
        entries = entries * block_levels(own_key, dims, cuts, -0.22, 0.18)
    return jnp.clip(entries, -most, most).astype(kind)


def setup_inputs(seed: int = 0) -> dict:
    splits = jax.random.split(jax.random.key(seed), 10)
    tokens = noise(splits[0], (REPLICAS, ROWS, MODEL_WIDTH), 1.0, 6.0, ((0, 16), (1, 16)))
    out_grad = noise(splits[1], (REPLICAS, ROWS, MODEL_WIDTH), 1.0, 6.0, ((0, 16), (1, 16)))
    routes_keys = jax.random.split(jax.random.fold_in(splits[2], 1), REPLICAS * ROWS // TOK_DEV)
    routes_turns = jax.random.permutation(jax.random.fold_in(splits[2], 3), REPLICAS * ROWS // TOK_DEV)
    routes = jax.vmap(lambda own, number: assign_block(jax.random.fold_in(splits[2], 2), own, number, TOK_DEV, EXPERT_TOTAL, TOP, CAP, 1))(routes_keys, routes_turns).reshape((REPLICAS, ROWS, TOP))
    route_weight = jnp.clip(0.19921875 + 0.80078125 * jax.random.uniform(splits[3], (REPLICAS, ROWS, TOP), jnp.float32) ** block_levels(splits[3], (REPLICAS, ROWS, TOP), ((0, 16), (1, 16)), -0.2, 0.2), 0.19921875, 1.0).astype(jnp.bfloat16)
    gate_up_matrix = noise(splits[4], (REPLICAS, EXPERT_TOTAL, MODEL_WIDTH, 2 * FF), 1.0, 6.0, ((0, 16), (1, 16)))
    down_matrix = noise(splits[5], (REPLICAS, EXPERT_TOTAL, MODEL_WIDTH, FF), 1.0, 6.0, ((0, 16), (1, 16)))
    gate_up_velocity = noise(splits[6], (REPLICAS, EXPERT_TOTAL, MODEL_WIDTH, 2 * FF), 1.0, 6.0, ((0, 16), (1, 16)))
    down_velocity = noise(splits[7], (REPLICAS, EXPERT_TOTAL, MODEL_WIDTH, FF), 1.0, 6.0, ((0, 16), (1, 16)))
    partner = draw_partner(jax.random.fold_in(splits[9], 71), 0)
    return {"tokens": tokens, "out_grad": out_grad, "routes": routes, "route_weight": route_weight, "gate_up_matrix": gate_up_matrix, "down_matrix": down_matrix, "gate_up_velocity": gate_up_velocity, "down_velocity": down_velocity, "partner": partner}


step_size = 0.2
momentum_decay = 0.9

def expert_gradient_pass(input_rows):
    input_buffer, gradient_buffer, gate_up_matrix, down_matrix, gate_up_velocity, down_velocity = input_rows
    inv_width = 1.0 / math.sqrt(MODEL_WIDTH)
    inverse_hidden = 1.0 / math.sqrt(FF)
    pre = jnp.dot(input_buffer, gate_up_matrix, preferred_element_type=jnp.float32) * inv_width
    gate = pre[:, :FF]
    up = pre[:, FF:]
    active = jax.nn.silu(gate)
    hidden_state = (active * up).astype(jnp.bfloat16)
    hidden_gradient = jnp.dot(gradient_buffer, down_matrix, preferred_element_type=jnp.float32) * inverse_hidden
    sigmoid_gate = jax.nn.sigmoid(gate)
    slope = sigmoid_gate * (1.0 + gate * (1.0 - sigmoid_gate))
    pre_grad = jnp.concatenate([hidden_gradient * up * slope, hidden_gradient * active], axis=1).astype(jnp.bfloat16)
    down_gradient = jnp.dot(gradient_buffer.T, hidden_state, preferred_element_type=jnp.float32) * inverse_hidden
    gate_up_grad = jnp.dot(input_buffer.T, pre_grad, preferred_element_type=jnp.float32) * inv_width
    paired_gradient = (jnp.dot(pre_grad, gate_up_matrix.T, preferred_element_type=jnp.float32) * inv_width).astype(jnp.bfloat16)
    next_gate_up = (gate_up_matrix.astype(jnp.float32) - step_size * (momentum_decay * gate_up_velocity.astype(jnp.float32) + gate_up_grad)).astype(jnp.bfloat16)
    next_down_matrix = (down_matrix.astype(jnp.float32) - step_size * (momentum_decay * down_velocity.astype(jnp.float32) + down_gradient)).astype(jnp.bfloat16)
    return (paired_gradient, next_gate_up, next_down_matrix)

def one_replica(input_rows):
    tokens, out_grad, routes, route_weight, gate_up_matrix, down_matrix, gate_up_velocity, down_velocity = input_rows
    buffered_rows = N_EXPERT * CAP
    flat_ids = routes.reshape(-1).astype(jnp.int32)
    pairs = flat_ids.shape[0]
    token_of = (jnp.arange(pairs, dtype=jnp.int32) // TOP).astype(jnp.int32)
    onehot = (flat_ids[:, None] == jnp.arange(EXPERT_TOTAL, dtype=jnp.int32)[None, :]).astype(jnp.int32)
    ranks = lax.optimization_barrier(jnp.sum((jnp.cumsum(onehot, axis=0) - onehot) * onehot, axis=1)).astype(jnp.int32)
    slot_lookup = (flat_ids * buffered_rows + ranks).astype(jnp.int32)
    row_inputs = tokens[token_of]
    scaled_rows = (out_grad[token_of].astype(jnp.float32) * route_weight.reshape(-1)[:, None].astype(jnp.float32)).astype(jnp.bfloat16)
    input_buffer = jnp.zeros((EXPERT_TOTAL * buffered_rows, MODEL_WIDTH), jnp.bfloat16).at[slot_lookup].set(row_inputs)
    gradient_buffer = jnp.zeros((EXPERT_TOTAL * buffered_rows, MODEL_WIDTH), jnp.bfloat16).at[slot_lookup].set(scaled_rows)
    paired_gradient, next_gate_up, next_down_matrix = lax.map(expert_gradient_pass, (input_buffer.reshape(EXPERT_TOTAL, buffered_rows, MODEL_WIDTH), gradient_buffer.reshape(EXPERT_TOTAL, buffered_rows, MODEL_WIDTH), gate_up_matrix, down_matrix, gate_up_velocity, down_velocity))
    gathered = paired_gradient.reshape(EXPERT_TOTAL * buffered_rows, MODEL_WIDTH)[slot_lookup]
    token_grad = lax.optimization_barrier(jnp.sum(gathered.astype(jnp.float32).reshape(-1, TOP, MODEL_WIDTH), axis=1)).astype(jnp.bfloat16)
    return (token_grad, next_gate_up, next_down_matrix)

def mix_pair(input_rows):
    own_weight, other_weight = input_rows
    return (0.5 * (own_weight.astype(jnp.float32) + other_weight.astype(jnp.float32))).astype(jnp.bfloat16)

def reference(tokens, out_grad, routes, route_weight, gate_up_matrix, down_matrix, gate_up_velocity, down_velocity, partner):
    token_grad, next_gate_up, next_down_matrix = lax.map(one_replica, (tokens, out_grad, routes, route_weight, gate_up_matrix, down_matrix, gate_up_velocity, down_velocity))
    mixed_gate_up = lax.map(mix_pair, (next_gate_up, next_gate_up[partner]))
    mixed_down = lax.map(mix_pair, (next_down_matrix, next_down_matrix[partner]))
    return (token_grad, mixed_gate_up, mixed_down)
```

```python
import functools
import math

import jax
import jax.numpy as jnp
from jax import lax
from jax.experimental import pallas as pl
from jax.experimental.pallas import tpu as pltpu
from jax.sharding import PartitionSpec as P

STEP = 0.2
DECAY = 0.9
MESH = pl.DeviceIdType.MESH
CHUNKS = 4
AHEAD = 3
BF16 = jnp.bfloat16
F32 = jnp.float32


def matmul(left, right, left_dim=1, right_dim=0):
    return lax.dot_general(
        left, right, (((left_dim,), (right_dim,)), ((), ())), preferred_element_type=F32
    )


def layer_kernel(
    shift,
    experts,
    info,
    tokens,
    grads,
    gate_up,
    down,
    gate_up_velocity,
    down_velocity,
    token_grad,
    mixed_gate_up,
    mixed_down,
    other_info,
    own_rows,
    other_rows,
    picks,
    packed,
    rows,
    w_gu,
    w_dn,
    v_gu,
    v_dn,
    factors,
    hidden,
    hidden_grad,
    pre_grad,
    new_gu,
    new_dn,
    far_gu,
    far_dn,
    returned,
    across,
    arrived,
    kept,
    load_sem,
    store_sem,
    z_send,
    z_recv,
    x_send,
    x_recv,
    ret_send,
    ret_recv,
    back_send,
    back_recv,
    mix_send,
    mix_recv,
):
    tok_rows, width = tokens.shape
    half_width = down.shape[1]
    group = experts // 2
    total = rows.shape[1]
    part_rows = total // 2
    capacity = part_rows // group
    columns = width // CHUNKS
    inv_width = 1.0 / math.sqrt(width)
    inv_hidden = 1.0 / math.sqrt(half_width)

    me = lax.axis_index("expert")
    replica = lax.axis_index("replica")
    side = me // group
    mine = me % group
    opposite = (me + group) % experts
    mate = replica + shift - 2 * shift * ((replica // shift) % 2)

    def member(at):
        return {"expert": side * group + at}

    def span(chunk):
        return pl.ds(chunk * columns, columns)

    def block(part, at):
        return pl.ds(pl.multiple_of(part * part_rows + at * capacity, capacity), capacity)

    barrier = pltpu.get_barrier_semaphore()
    for step in range(1, group):
        pl.semaphore_signal(
            barrier, inc=1, device_id=member((mine + step) % group), device_id_type=MESH
        )
    pl.semaphore_signal(barrier, inc=1, device_id={"expert": opposite}, device_id_type=MESH)
    pl.semaphore_signal(barrier, inc=1, device_id={"replica": mate}, device_id_type=MESH)

    sources = (tokens, grads)
    loads = [
        pltpu.make_async_copy(tokens, own_rows.at[0], load_sem.at[0]),
        pltpu.make_async_copy(grads, own_rows.at[1], load_sem.at[1]),
        pltpu.make_async_copy(gate_up, w_gu, load_sem.at[2]),
        pltpu.make_async_copy(down, w_dn, load_sem.at[3]),
        pltpu.make_async_copy(down_velocity, v_dn, load_sem.at[4]),
        pltpu.make_async_copy(gate_up_velocity, v_gu, load_sem.at[5]),
    ]
    for load in loads:
        load.start()
    pl.semaphore_wait(barrier, group + 1)

    def z_copy(index):
        array, chunk = divmod(index, CHUNKS)
        return pltpu.make_async_remote_copy(
            src_ref=sources[array].at[:, span(chunk)],
            dst_ref=other_rows.at[array, :, span(chunk)],
            send_sem=z_send.at[index],
            recv_sem=z_recv.at[index],
            device_id={"expert": opposite},
            device_id_type=MESH,
        )

    info_copy = pltpu.make_async_remote_copy(
        src_ref=info,
        dst_ref=other_info,
        send_sem=z_send.at[2 * CHUNKS],
        recv_sem=z_recv.at[2 * CHUNKS],
        device_id={"expert": opposite},
        device_id_type=MESH,
    )
    info_copy.start()
    for index in range(AHEAD):
        z_copy(index).start()

    def choose(part, table):
        names = [table[k : k + 1, :] for k in range(2)]
        weights = [table[2 + k : 3 + k, :] for k in range(2)]
        listed = lax.broadcasted_iota(jnp.int32, (experts, tok_rows), 0).astype(F32)
        member_of = jnp.where((names[0] == listed) | (names[1] == listed), 1.0, 0.0)
        earlier = jnp.where(
            lax.broadcasted_iota(jnp.int32, (tok_rows, tok_rows), 0)
            < lax.broadcasted_iota(jnp.int32, (tok_rows, tok_rows), 1),
            1.0,
            0.0,
        )
        before = matmul(member_of.astype(BF16), earlier.astype(BF16))
        first = (side * part_rows).astype(F32)
        slots = [
            name * float(capacity)
            + jnp.sum(jnp.where(name == listed, before, 0.0), axis=0, keepdims=True)
            - first
            for name in names
        ]
        place = lax.broadcasted_iota(jnp.int32, (part_rows, tok_rows), 0).astype(F32)
        hits = [slot == place for slot in slots]
        picks[0, part] = jnp.where(hits[0] | hits[1], 1.0, 0.0).astype(BF16)
        picks[1, part] = (
            jnp.where(hits[0], weights[0], 0.0) + jnp.where(hits[1], weights[1], 0.0)
        ).astype(BF16)

    def pass_on(source, target, part, chunk, send, recv):
        target[block(part, mine), span(chunk)] = source[block(part, mine), span(chunk)]
        for step in range(1, group):
            at = (mine + step) % group
            pltpu.make_async_remote_copy(
                src_ref=source.at[block(part, at), span(chunk)],
                dst_ref=target.at[block(part, mine), span(chunk)],
                send_sem=send,
                recv_sem=recv,
                device_id=member(at),
                device_id_type=MESH,
            ).start()

    def all_sent_or_here(source, target, cut, send, recv):
        some = pl.ds(0, part_rows - capacity)
        return pltpu.make_async_remote_copy(
            src_ref=source.at[some, cut],
            dst_ref=target.at[some, cut],
            send_sem=send,
            recv_sem=recv,
            device_id={"expert": opposite},
            device_id_type=MESH,
        )

    def dispatch(array, part, chunk):
        held = own_rows if part == 0 else other_rows
        picked = matmul(picks[array, part], held[array, :, span(chunk)])
        packed[array, part * part_rows : (part + 1) * part_rows, span(chunk)] = picked.astype(BF16)
        pass_on(
            packed.at[array],
            rows.at[array],
            part,
            chunk,
            x_send.at[2 * array + part],
            x_recv.at[(2 * array + part) * CHUNKS + chunk],
        )

    def wait_rows(array, part, chunk):
        all_sent_or_here(
            packed.at[array],
            rows.at[array],
            span(chunk),
            x_send.at[2 * array + part],
            x_recv.at[(2 * array + part) * CHUNKS + chunk],
        ).wait_recv()

    def forward(part):
        def one(at, carry):
            here = pl.ds(pl.multiple_of(part * part_rows + at * 128, 128), 128)
            pre = matmul(rows[0, here, :], w_gu[...]) * inv_width
            gate = pre[:, :half_width]
            upper = pre[:, half_width:]
            sigmoid = jax.nn.sigmoid(gate)
            active = gate * sigmoid
            hidden[here, :] = (active * upper).astype(BF16)
            factors[here, :half_width] = upper * (sigmoid * (1.0 + gate * (1.0 - sigmoid)))
            factors[here, half_width:] = active
            return carry

        lax.fori_loop(0, part_rows // 128, one, 0)

    choose(0, info)
    loads[0].wait()
    for chunk in range(CHUNKS):
        dispatch(0, 0, chunk)
    loads[1].wait()
    for chunk in range(CHUNKS):
        dispatch(1, 0, chunk)
    info_copy.wait()
    choose(1, other_info)

    def take(index):
        copy = z_copy(index)
        copy.wait_recv()
        copy.wait_send()
        if index + AHEAD < 2 * CHUNKS:
            z_copy(index + AHEAD).start()
        dispatch(index // CHUNKS, 1, index % CHUNKS)

    for index in range(CHUNKS):
        take(index)
        if index == CHUNKS - 2:
            loads[2].wait()
            for chunk in range(CHUNKS):
                wait_rows(0, 0, chunk)
            forward(0)
    loads[3].wait()
    loads[4].wait()
    loads[5].wait()

    def swap_copy(source, target, at, count, index):
        part = pl.ds(at * count, count)
        return pltpu.make_async_remote_copy(
            src_ref=source.at[part],
            dst_ref=target.at[part],
            send_sem=mix_send.at[index],
            recv_sem=mix_recv.at[index],
            device_id={"replica": mate},
            device_id_type=MESH,
        )

    def stepped(weight, velocity, gradient):
        return (
            weight.astype(F32) - STEP * (DECAY * velocity.astype(F32) + gradient)
        ).astype(BF16)

    def down_chunk(chunk):
        wait_rows(1, 0, chunk)
        wait_rows(1, 1, chunk)
        here = pl.ds(chunk * columns, columns)

        def one(at, carry):
            those = pl.ds(pl.multiple_of(at * 256, 256), 256)
            term = matmul(rows[1, those, span(chunk)], w_dn[here, :])
            if chunk == 0:
                hidden_grad[those, :] = term
            else:
                hidden_grad[those, :] += term
            return carry

        lax.fori_loop(0, total // 256, one, 0)
        gradient = matmul(rows[1, :, span(chunk)], hidden[...], 0, 0) * inv_hidden
        new_dn[here, :] = stepped(w_dn[here, :], v_dn[here, :], gradient)
        swap_copy(new_dn, far_dn, chunk, columns, CHUNKS + chunk).start()

    for index in range(CHUNKS):
        take(CHUNKS + index)
        if index == 1:
            for chunk in range(CHUNKS):
                wait_rows(0, 1, chunk)
            forward(1)
        if index >= 2:
            down_chunk(index - 2)
    for chunk in range(CHUNKS - 2, CHUNKS):
        down_chunk(chunk)

    def finish(at, carry):
        here = pl.ds(pl.multiple_of(at * 128, 128), 128)
        scaled = hidden_grad[here, :] * inv_hidden
        pre_grad[here, :half_width] = (scaled * factors[here, :half_width]).astype(BF16)
        pre_grad[here, half_width:] = (scaled * factors[here, half_width:]).astype(BF16)
        return carry

    lax.fori_loop(0, total // 128, finish, 0)

    for part in range(2):
        all_sent_or_here(
            packed.at[0], rows.at[0], slice(None), x_send.at[part], x_recv.at[0]
        ).wait_send()

    def give_back(part, chunk):
        here = pl.ds(chunk * columns, columns)
        base = part * part_rows

        def one(at, carry):
            those = pl.ds(pl.multiple_of(base + at * 256, 256), 256)
            pair = matmul(pre_grad[those, :], w_gu[here, :], 1, 1) * inv_width
            packed[0, those, span(chunk)] = pair.astype(BF16)
            return carry

        lax.fori_loop(0, part_rows // 256, one, 0)
        pass_on(
            packed.at[0],
            returned,
            part,
            chunk,
            ret_send.at[part],
            ret_recv.at[part * CHUNKS + chunk],
        )

    def gate_up_chunk(chunk):
        here = pl.ds(chunk * columns, columns)
        gradient = matmul(rows[0, :, span(chunk)], pre_grad[...], 0, 0) * inv_width
        new_gu[here, :] = stepped(w_gu[here, :], v_gu[here, :], gradient)
        swap_copy(new_gu, far_gu, chunk, columns, chunk).start()

    for chunk in range(CHUNKS):
        give_back(1, chunk)
        gate_up_chunk(chunk)

    def wait_back(part, chunk):
        all_sent_or_here(
            packed.at[0],
            returned,
            span(chunk),
            ret_send.at[part],
            ret_recv.at[part * CHUNKS + chunk],
        ).wait_recv()

    def combine(part, chunk):
        wait_back(part, chunk)
        there = returned[part * part_rows : (part + 1) * part_rows, span(chunk)]
        return matmul(picks[0, part], there, 0, 0).astype(BF16)

    def back_copy(chunk):
        return pltpu.make_async_remote_copy(
            src_ref=across.at[:, span(chunk)],
            dst_ref=arrived.at[:, span(chunk)],
            send_sem=back_send.at[chunk],
            recv_sem=back_recv.at[chunk],
            device_id={"expert": opposite},
            device_id_type=MESH,
        )

    for chunk in range(CHUNKS):
        across[:, span(chunk)] = combine(1, chunk)
        back_copy(chunk).start()
        give_back(0, chunk)
    for chunk in range(CHUNKS):
        kept[:, span(chunk)] = combine(0, chunk)

    stores = []

    def mix(own, far, result, chunk, index):
        copy = swap_copy(own, far, chunk, columns, index)
        copy.wait_recv()
        here = pl.ds(chunk * columns, columns)
        far[here, :] = (0.5 * (own[here, :].astype(F32) + far[here, :].astype(F32))).astype(BF16)
        store = pltpu.make_async_copy(far.at[here], result.at[here], store_sem.at[index])
        store.start()
        stores.append(store)
        copy.wait_send()

    for chunk in range(CHUNKS):
        mix(new_dn, far_dn, mixed_down, chunk, CHUNKS + chunk)
    for chunk in range(CHUNKS):
        mix(new_gu, far_gu, mixed_gate_up, chunk, chunk)
    for chunk in range(CHUNKS):
        copy = back_copy(chunk)
        copy.wait_recv()
        both = kept[:, span(chunk)].astype(F32) + arrived[:, span(chunk)].astype(F32)
        kept[:, span(chunk)] = both.astype(BF16)
        store = pltpu.make_async_copy(
            kept.at[:, span(chunk)], token_grad.at[:, span(chunk)], store_sem.at[2 * CHUNKS + chunk]
        )
        store.start()
        stores.append(store)
        copy.wait_send()
    for part in range(2):
        all_sent_or_here(
            packed.at[1], rows.at[1], slice(None), x_send.at[2 + part], x_recv.at[0]
        ).wait_send()
        all_sent_or_here(
            packed.at[0], returned, slice(None), ret_send.at[part], ret_recv.at[0]
        ).wait_send()
    for store in stores:
        store.wait()


def layer(level, experts, info, *arrays):
    tokens, _, gate_up, down = arrays[:4]
    tok_rows, width = tokens.shape
    twice = gate_up.shape[1]
    single = down.shape[1]
    total = 2 * tok_rows * 2
    part_rows = total // 2
    vmem = pltpu.VMEM
    sems = pltpu.SemaphoreType.DMA
    anywhere = pl.BlockSpec(memory_space=pl.ANY)
    return pl.pallas_call(
        functools.partial(layer_kernel, 1 << level, experts),
        out_shape=(
            jax.ShapeDtypeStruct((tok_rows, width), BF16),
            jax.ShapeDtypeStruct((width, twice), BF16),
            jax.ShapeDtypeStruct((width, single), BF16),
        ),
        in_specs=[pl.BlockSpec(memory_space=pltpu.VMEM)] + [anywhere] * 6,
        out_specs=(anywhere,) * 3,
        scratch_shapes=[
            vmem(info.shape, F32),
            vmem((2, tok_rows, width), BF16),
            vmem((2, tok_rows, width), BF16),
            vmem((2, 2, part_rows, tok_rows), BF16),
            vmem((2, total, width), BF16),
            vmem((2, total, width), BF16),
            vmem((width, twice), BF16),
            vmem((width, single), BF16),
            vmem((width, twice), BF16),
            vmem((width, single), BF16),
            vmem((total, twice), F32),
            vmem((total, single), BF16),
            vmem((total, single), F32),
            vmem((total, twice), BF16),
            vmem((width, twice), BF16),
            vmem((width, single), BF16),
            vmem((width, twice), BF16),
            vmem((width, single), BF16),
            vmem((total, width), BF16),
            vmem((tok_rows, width), BF16),
            vmem((tok_rows, width), BF16),
            vmem((tok_rows, width), BF16),
            sems((6,)),
            sems((3 * CHUNKS,)),
            sems((2 * CHUNKS + 1,)),
            sems((2 * CHUNKS + 1,)),
            sems((4,)),
            sems((4 * CHUNKS,)),
            sems((2,)),
            sems((2 * CHUNKS,)),
            sems((CHUNKS,)),
            sems((CHUNKS,)),
            sems((2 * CHUNKS,)),
            sems((2 * CHUNKS,)),
        ],
        name=f"layer_shift_{1 << level}",
        compiler_params=pltpu.CompilerParams(
            collective_id=level, has_side_effects=True, vmem_limit_bytes=60 << 20
        ),
    )(info, *arrays)


def per_device(
    tokens,
    out_grad,
    routes,
    route_weight,
    gate_up_matrix,
    down_matrix,
    gate_up_velocity,
    down_velocity,
    partner,
):
    experts = lax.axis_size("expert")
    levels = lax.axis_size("replica").bit_length() - 1
    info = jnp.concatenate(
        [
            routes[0].T.astype(F32),
            route_weight[0].T.astype(F32),
            jnp.zeros((4, tokens.shape[1]), F32),
        ],
        axis=0,
    )
    shift = partner[0]
    level = jnp.zeros((), jnp.int32)
    for bit in range(levels):
        level = level + bit * jnp.bitwise_and(jnp.right_shift(shift, bit), 1)
    token_grad, mixed_gate_up, mixed_down = lax.switch(
        level,
        [functools.partial(layer, at, experts) for at in range(levels)],
        info,
        tokens[0],
        out_grad[0],
        gate_up_matrix[0, 0],
        down_matrix[0, 0],
        gate_up_velocity[0, 0],
        down_velocity[0, 0],
    )
    return token_grad[None], mixed_gate_up[None, None], mixed_down[None, None]


def solution(mesh):
    row = P("replica", "expert", None)
    weight = P("replica", "expert", None, None)
    return jax.shard_map(
        per_device,
        mesh=mesh,
        in_specs=(row,) * 4 + (weight,) * 4 + (P(),),
        out_specs=(row, weight, weight),
        check_vma=False,
    )
```

```python
import functools
import math

import jax
import jax.numpy as jnp
from jax import lax
from jax.experimental import pallas as pl
from jax.experimental.pallas import tpu as pltpu
from jax.sharding import PartitionSpec as P

STEP = 0.2
DECAY = 0.9
MESH = pl.DeviceIdType.MESH
CHUNKS = 4
AHEAD = 3
FIRST = 2
FORWARD_GAP = 3
LATE = 6
BF16 = jnp.bfloat16
F32 = jnp.float32


def matmul(left, right, left_dim=1, right_dim=0):
    return lax.dot_general(
        left, right, (((left_dim,), (right_dim,)), ((), ())), preferred_element_type=F32
    )


def layer_kernel(
    shift,
    experts,
    info,
    tokens,
    grads,
    gate_up,
    down,
    gate_up_velocity,
    down_velocity,
    token_grad,
    mixed_gate_up,
    mixed_down,
    other_info,
    held,
    picks,
    packed,
    rows,
    w_gu,
    w_dn,
    v_gu,
    v_dn,
    factors,
    hidden,
    hidden_grad,
    pre_grad,
    new_gu,
    new_dn,
    far_gu,
    far_dn,
    returned,
    across,
    arrived,
    load_sem,
    store_sem,
    z_send,
    z_recv,
    x_send,
    x_recv,
    ret_send,
    ret_recv,
    back_send,
    back_recv,
    mix_send,
    mix_recv,
):
    tok_rows, width = tokens.shape
    half_width = down.shape[1]
    group = experts // 2
    total = rows.shape[1]
    part_rows = total // 2
    capacity = part_rows // group
    columns = width // CHUNKS
    inv_width = 1.0 / math.sqrt(width)
    inv_hidden = 1.0 / math.sqrt(half_width)

    me = lax.axis_index("expert")
    replica = lax.axis_index("replica")
    side = me // group
    mine = me % group
    opposite = (me + group) % experts
    mate = replica + shift - 2 * shift * ((replica // shift) % 2)

    def member(at):
        return {"expert": side * group + at}

    def span(chunk):
        return pl.ds(pl.multiple_of(chunk * columns, columns), columns)

    def block(part, at):
        return pl.ds(pl.multiple_of(part * part_rows + at * capacity, capacity), capacity)

    barrier = pltpu.get_barrier_semaphore()
    for step in range(1, group):
        pl.semaphore_signal(
            barrier, inc=1, device_id=member((mine + step) % group), device_id_type=MESH
        )
    pl.semaphore_signal(barrier, inc=1, device_id={"expert": opposite}, device_id_type=MESH)
    pl.semaphore_signal(barrier, inc=1, device_id={"replica": mate}, device_id_type=MESH)

    loads = [
        pltpu.make_async_copy(tokens, held.at[0, 0], load_sem.at[0]),
        pltpu.make_async_copy(grads, held.at[0, 1], load_sem.at[1]),
        pltpu.make_async_copy(gate_up, w_gu, load_sem.at[2]),
        pltpu.make_async_copy(down, w_dn, load_sem.at[3]),
        pltpu.make_async_copy(down_velocity, v_dn, load_sem.at[4]),
        pltpu.make_async_copy(gate_up_velocity, v_gu, load_sem.at[5]),
    ]
    for load in loads:
        load.start()
    pl.semaphore_wait(barrier, group + 1)

    def z_copy(index, source=None):
        array, chunk = index // CHUNKS, index % CHUNKS
        source = held.at[0, array] if source is None else source
        return pltpu.make_async_remote_copy(
            src_ref=source.at[:, span(chunk)],
            dst_ref=held.at[1, array, :, span(chunk)],
            send_sem=z_send.at[index],
            recv_sem=z_recv.at[index],
            device_id={"expert": opposite},
            device_id_type=MESH,
        )

    info_copy = pltpu.make_async_remote_copy(
        src_ref=info,
        dst_ref=other_info,
        send_sem=z_send.at[2 * CHUNKS],
        recv_sem=z_recv.at[2 * CHUNKS],
        device_id={"expert": opposite},
        device_id_type=MESH,
    )
    info_copy.start()
    for index in range(AHEAD):
        z_copy(index, tokens).start()

    def choose(part, table):
        names = [table[k : k + 1, :] for k in range(2)]
        weights = [table[2 + k : 3 + k, :] for k in range(2)]
        listed = lax.broadcasted_iota(jnp.int32, (experts, tok_rows), 0).astype(F32)
        member_of = jnp.where((names[0] == listed) | (names[1] == listed), 1.0, 0.0)
        earlier = jnp.where(
            lax.broadcasted_iota(jnp.int32, (tok_rows, tok_rows), 0)
            < lax.broadcasted_iota(jnp.int32, (tok_rows, tok_rows), 1),
            1.0,
            0.0,
        )
        before = matmul(member_of.astype(BF16), earlier.astype(BF16))
        first = (side * part_rows).astype(F32)
        slots = [
            name * float(capacity)
            + jnp.sum(jnp.where(name == listed, before, 0.0), axis=0, keepdims=True)
            - first
            for name in names
        ]
        place = lax.broadcasted_iota(jnp.int32, (part_rows, tok_rows), 0).astype(F32)
        hits = [slot == place for slot in slots]
        picks[0, part] = jnp.where(hits[0] | hits[1], 1.0, 0.0).astype(BF16)
        picks[1, part] = (
            jnp.where(hits[0], weights[0], 0.0) + jnp.where(hits[1], weights[1], 0.0)
        ).astype(BF16)

    def pass_on(source, target, part, chunk, send, recv):
        target[block(part, mine), span(chunk)] = source[block(part, mine), span(chunk)]

        def one(step, carry):
            at = (mine + step) % group
            pltpu.make_async_remote_copy(
                src_ref=source.at[block(part, at), span(chunk)],
                dst_ref=target.at[block(part, mine), span(chunk)],
                send_sem=send,
                recv_sem=recv,
                device_id=member(at),
                device_id_type=MESH,
            ).start()
            return carry

        lax.fori_loop(1, group, one, 0)

    def all_sent_or_here(source, target, cut, send, recv):
        some = pl.ds(0, part_rows - capacity)
        return pltpu.make_async_remote_copy(
            src_ref=source.at[some, cut],
            dst_ref=target.at[some, cut],
            send_sem=send,
            recv_sem=recv,
            device_id={"expert": opposite},
            device_id_type=MESH,
        )

    def half_rows(part, at, count):
        return pl.ds(pl.multiple_of(part * part_rows + at * count, count), count)

    def dispatch(array, part, chunk):
        def one(at, carry):
            slots = pl.ds(pl.multiple_of(at * 128, 128), 128)
            picked = matmul(picks[array, part, slots, :], held[part, array, :, span(chunk)])
            packed[array, half_rows(part, at, 128), span(chunk)] = picked.astype(BF16)
            return carry

        lax.fori_loop(0, part_rows // 128, one, 0)
        pass_on(
            packed.at[array],
            rows.at[array],
            part,
            chunk,
            x_send.at[2 * array + part],
            x_recv.at[(2 * array + part) * CHUNKS + chunk],
        )

    def wait_rows(array, part, chunk):
        all_sent_or_here(
            packed.at[array],
            rows.at[array],
            span(chunk),
            x_send.at[2 * array + part],
            x_recv.at[(2 * array + part) * CHUNKS + chunk],
        ).wait_recv()

    def each(count, step):
        def one(at, carry):
            step(at)
            return carry

        lax.fori_loop(0, count, one, 0)

    def forward(part):
        each(CHUNKS, lambda chunk: wait_rows(0, part, chunk))

        def one(at):
            here = half_rows(part, at, 128)
            pre = matmul(rows[0, here, :], w_gu[...]) * inv_width
            gate = pre[:, :half_width]
            upper = pre[:, half_width:]
            sigmoid = jax.nn.sigmoid(gate)
            active = gate * sigmoid
            hidden[here, :] = (active * upper).astype(BF16)
            factors[here, :half_width] = upper * (sigmoid * (1.0 + gate * (1.0 - sigmoid)))
            factors[here, half_width:] = active
            hidden_grad[here, :] = jnp.zeros((128, half_width), F32)

        each(part_rows // 128, one)

    choose(0, info)
    loads[0].wait()
    loads[1].wait()
    each(2 * CHUNKS, lambda index: dispatch(index // CHUNKS, 0, index % CHUNKS))
    info_copy.wait()
    choose(1, other_info)
    for load in loads[2:]:
        load.wait()

    def take(index):
        copy = z_copy(index)
        copy.wait_recv()
        copy.wait_send()

        @pl.when(index + AHEAD < 2 * CHUNKS)
        def _():
            z_copy(index + AHEAD).start()

        dispatch(index // CHUNKS, 1, index % CHUNKS)

    def swap_copy(source, target, at, count, index):
        part = pl.ds(pl.multiple_of(at * count, count), count)
        return pltpu.make_async_remote_copy(
            src_ref=source.at[part],
            dst_ref=target.at[part],
            send_sem=mix_send.at[index],
            recv_sem=mix_recv.at[index],
            device_id={"replica": mate},
            device_id_type=MESH,
        )

    def stepped(weight, velocity, gradient):
        return (
            weight.astype(F32) - STEP * (DECAY * velocity.astype(F32) + gradient)
        ).astype(BF16)

    def down_chunk(chunk):
        wait_rows(1, 0, chunk)
        wait_rows(1, 1, chunk)

        def term(at):
            those = pl.ds(pl.multiple_of(at * 256, 256), 256)
            hidden_grad[those, :] += matmul(rows[1, those, span(chunk)], w_dn[span(chunk), :])

        each(total // 256, term)

        def update(at):
            here = pl.ds(pl.multiple_of(chunk * columns + at * 256, 256), 256)
            gradient = matmul(rows[1, :, here], hidden[...], 0, 0) * inv_hidden
            new_dn[here, :] = stepped(w_dn[here, :], v_dn[here, :], gradient)

        each(columns // 256, update)
        swap_copy(new_dn, far_dn, chunk, columns, CHUNKS + chunk).start()

    def dispatch_step(index):
        @pl.when(index < 2 * CHUNKS)
        def _():
            take(index)

        @pl.when((index == FIRST) | (index == FIRST + FORWARD_GAP))
        def _():
            forward((index - FIRST) // FORWARD_GAP)

        @pl.when(index >= LATE)
        def _():
            down_chunk(index - LATE)

    each(LATE + CHUNKS, dispatch_step)

    def finish(at):
        here = pl.ds(pl.multiple_of(at * 128, 128), 128)
        scaled = hidden_grad[here, :] * inv_hidden
        pre_grad[here, :half_width] = (scaled * factors[here, :half_width]).astype(BF16)
        pre_grad[here, half_width:] = (scaled * factors[here, half_width:]).astype(BF16)

    each(total // 128, finish)

    for part in range(2):
        all_sent_or_here(
            packed.at[0], rows.at[0], slice(None), x_send.at[part], x_recv.at[0]
        ).wait_send()

    def give_back(part, chunk):
        def one(at):
            those = half_rows(part, at, 256)
            pair = matmul(pre_grad[those, :], w_gu[span(chunk), :], 1, 1) * inv_width
            packed[0, those, span(chunk)] = pair.astype(BF16)

        each(part_rows // 256, one)
        pass_on(
            packed.at[0],
            returned,
            part,
            chunk,
            ret_send.at[part],
            ret_recv.at[part * CHUNKS + chunk],
        )

    def gate_up_chunk(chunk):
        def update(at):
            here = pl.ds(pl.multiple_of(chunk * columns + at * 256, 256), 256)
            gradient = matmul(rows[0, :, here], pre_grad[...], 0, 0) * inv_width
            new_gu[here, :] = stepped(w_gu[here, :], v_gu[here, :], gradient)

        each(columns // 256, update)
        swap_copy(new_gu, far_gu, chunk, columns, chunk).start()

    def wait_back(part, chunk):
        all_sent_or_here(
            packed.at[0],
            returned,
            span(chunk),
            ret_send.at[part],
            ret_recv.at[part * CHUNKS + chunk],
        ).wait_recv()

    def combine(part, chunk):
        wait_back(part, chunk)
        there = returned[half_rows(part, 0, part_rows), span(chunk)]
        across[part, :, span(chunk)] = matmul(picks[0, part], there, 0, 0).astype(BF16)

    def back_copy(chunk):
        return pltpu.make_async_remote_copy(
            src_ref=across.at[1, :, span(chunk)],
            dst_ref=arrived.at[:, span(chunk)],
            send_sem=back_send.at[chunk],
            recv_sem=back_recv.at[chunk],
            device_id={"expert": opposite},
            device_id_type=MESH,
        )

    def return_step(index):
        @pl.when(index < 2 * CHUNKS)
        def _():
            give_back(1 - index // CHUNKS, index % CHUNKS)

        @pl.when(index < CHUNKS)
        def _():
            gate_up_chunk(index)

        @pl.when(index >= CHUNKS)
        def _():
            combine(2 - index // CHUNKS, index % CHUNKS)

        @pl.when((index >= CHUNKS) & (index < 2 * CHUNKS))
        def _():
            back_copy(index % CHUNKS).start()

    each(3 * CHUNKS, return_step)

    def mix(own, far, result, chunk, index):
        copy = swap_copy(own, far, chunk, columns, index)
        copy.wait_recv()
        here = span(chunk)
        far[here, :] = (0.5 * (own[here, :].astype(F32) + far[here, :].astype(F32))).astype(BF16)
        pltpu.make_async_copy(far.at[here], result.at[here], store_sem.at[index]).start()
        copy.wait_send()

    each(CHUNKS, lambda chunk: mix(new_dn, far_dn, mixed_down, chunk, CHUNKS + chunk))
    each(CHUNKS, lambda chunk: mix(new_gu, far_gu, mixed_gate_up, chunk, chunk))

    def total_up(chunk):
        copy = back_copy(chunk)
        copy.wait_recv()
        here = span(chunk)
        both = across[0, :, here].astype(F32) + arrived[:, here].astype(F32)
        arrived[:, here] = both.astype(BF16)
        pltpu.make_async_copy(
            arrived.at[:, here], token_grad.at[:, here], store_sem.at[2 * CHUNKS + chunk]
        ).start()
        copy.wait_send()

    each(CHUNKS, total_up)
    for part in range(2):
        all_sent_or_here(
            packed.at[1], rows.at[1], slice(None), x_send.at[2 + part], x_recv.at[0]
        ).wait_send()
        all_sent_or_here(
            packed.at[0], returned, slice(None), ret_send.at[part], ret_recv.at[0]
        ).wait_send()

    def stored(chunk):
        here = span(chunk)
        for own, result, index in (
            (far_dn.at[here], mixed_down.at[here], CHUNKS + chunk),
            (far_gu.at[here], mixed_gate_up.at[here], chunk),
            (arrived.at[:, here], token_grad.at[:, here], 2 * CHUNKS + chunk),
        ):
            pltpu.make_async_copy(own, result, store_sem.at[index]).wait()

    each(CHUNKS, stored)


def layer(level, experts, info, *arrays):
    tokens, _, gate_up, down = arrays[:4]
    tok_rows, width = tokens.shape
    twice = gate_up.shape[1]
    single = down.shape[1]
    total = 2 * tok_rows * 2
    part_rows = total // 2
    vmem = pltpu.VMEM
    sems = pltpu.SemaphoreType.DMA
    anywhere = pl.BlockSpec(memory_space=pl.ANY)
    return pl.pallas_call(
        functools.partial(layer_kernel, 1 << level, experts),
        out_shape=(
            jax.ShapeDtypeStruct((tok_rows, width), BF16),
            jax.ShapeDtypeStruct((width, twice), BF16),
            jax.ShapeDtypeStruct((width, single), BF16),
        ),
        in_specs=[pl.BlockSpec(memory_space=pltpu.VMEM)] + [anywhere] * 6,
        out_specs=(anywhere,) * 3,
        scratch_shapes=[
            vmem(info.shape, F32),
            vmem((2, 2, tok_rows, width), BF16),
            vmem((2, 2, part_rows, tok_rows), BF16),
            vmem((2, total, width), BF16),
            vmem((2, total, width), BF16),
            vmem((width, twice), BF16),
            vmem((width, single), BF16),
            vmem((width, twice), BF16),
            vmem((width, single), BF16),
            vmem((total, twice), F32),
            vmem((total, single), BF16),
            vmem((total, single), F32),
            vmem((total, twice), BF16),
            vmem((width, twice), BF16),
            vmem((width, single), BF16),
            vmem((width, twice), BF16),
            vmem((width, single), BF16),
            vmem((total, width), BF16),
            vmem((2, tok_rows, width), BF16),
            vmem((tok_rows, width), BF16),
            sems((6,)),
            sems((3 * CHUNKS,)),
            sems((2 * CHUNKS + 1,)),
            sems((2 * CHUNKS + 1,)),
            sems((4,)),
            sems((4 * CHUNKS,)),
            sems((2,)),
            sems((2 * CHUNKS,)),
            sems((CHUNKS,)),
            sems((CHUNKS,)),
            sems((2 * CHUNKS,)),
            sems((2 * CHUNKS,)),
        ],
        name=f"layer_shift_{1 << level}",
        compiler_params=pltpu.CompilerParams(
            collective_id=level, has_side_effects=True, vmem_limit_bytes=60 << 20
        ),
    )(info, *arrays)


def per_device(
    tokens,
    out_grad,
    routes,
    route_weight,
    gate_up_matrix,
    down_matrix,
    gate_up_velocity,
    down_velocity,
    partner,
):
    experts = lax.axis_size("expert")
    levels = lax.axis_size("replica").bit_length() - 1
    info = jnp.concatenate(
        [
            routes[0].T.astype(F32),
            route_weight[0].T.astype(F32),
            jnp.zeros((4, tokens.shape[1]), F32),
        ],
        axis=0,
    )
    shift = partner[0]
    level = jnp.zeros((), jnp.int32)
    for bit in range(levels):
        level = level + bit * jnp.bitwise_and(jnp.right_shift(shift, bit), 1)
    token_grad, mixed_gate_up, mixed_down = lax.switch(
        level,
        [functools.partial(layer, at, experts) for at in range(levels)],
        info,
        tokens[0],
        out_grad[0],
        gate_up_matrix[0, 0],
        down_matrix[0, 0],
        gate_up_velocity[0, 0],
        down_velocity[0, 0],
    )
    return token_grad[None], mixed_gate_up[None, None], mixed_down[None, None]


def solution(mesh):
    row = P("replica", "expert", None)
    weight = P("replica", "expert", None, None)
    return jax.shard_map(
        per_device,
        mesh=mesh,
        in_specs=(row,) * 4 + (weight,) * 4 + (P(),),
        out_specs=(row, weight, weight),
        check_vma=False,
    )
```

```python
import functools
import math

import jax
import jax.numpy as jnp
from jax import lax
from jax.experimental import pallas as pl
from jax.experimental.pallas import tpu as pltpu
from jax.sharding import PartitionSpec as P

STEP = 0.2
DECAY = 0.9
MESH = pl.DeviceIdType.MESH
CHUNKS = 8
FIRST = 8
FORWARD_GAP = 2
LATE = 10
LAG = 3
BF16 = jnp.bfloat16
F32 = jnp.float32


def matmul(left, right, left_dim=1, right_dim=0):
    return lax.dot_general(
        left, right, (((left_dim,), (right_dim,)), ((), ())), preferred_element_type=F32
    )


def layer_kernel(
    shift,
    experts,
    names,
    shares,
    tokens,
    grads,
    gate_up,
    down,
    gate_up_velocity,
    down_velocity,
    out_gu,
    far_gu,
    out_dn,
    far_dn,
    kept,
    arrived,
    info,
    other_info,
    held,
    picks,
    packed,
    rows,
    w_gu,
    w_dn,
    v_gu,
    v_dn,
    factors,
    hidden,
    hidden_grad,
    pre_grad,
    new_gu,
    new_dn,
    returned,
    across,
    load_sem,
    store_sem,
    z_send,
    z_recv,
    x_send,
    x_recv,
    ret_send,
    ret_recv,
    back_send,
    back_recv,
    mix_send,
    mix_recv,
):
    tok_rows, width = tokens.shape
    half_width = down.shape[1]
    group = experts // 2
    total = rows.shape[1]
    part_rows = total // 2
    capacity = part_rows // group
    columns = width // CHUNKS
    inv_width = 1.0 / math.sqrt(width)
    inv_hidden = 1.0 / math.sqrt(half_width)

    me = lax.axis_index("expert")
    replica = lax.axis_index("replica")
    side = me // group
    mine = me % group
    opposite = (me + group) % experts
    mate = replica + shift - 2 * shift * ((replica // shift) % 2)

    def member(at):
        return {"expert": side * group + at}

    def span(chunk):
        return pl.ds(pl.multiple_of(chunk * columns, columns), columns)

    def block(part, at):
        return pl.ds(pl.multiple_of(part * part_rows + at * capacity, capacity), capacity)

    info[...] = jnp.zeros_like(info)
    info[0:2, :] = names[...].astype(F32)
    info[2:4, :] = shares[...].astype(F32)

    barrier = pltpu.get_barrier_semaphore()
    for step in range(1, group):
        pl.semaphore_signal(
            barrier, inc=1, device_id=member((mine + step) % group), device_id_type=MESH
        )
    pl.semaphore_signal(barrier, inc=1, device_id={"expert": opposite}, device_id_type=MESH)
    pl.semaphore_signal(barrier, inc=1, device_id={"replica": mate}, device_id_type=MESH)

    loads = [
        pltpu.make_async_copy(tokens, held.at[0, 0], load_sem.at[0]),
        pltpu.make_async_copy(grads, held.at[0, 1], load_sem.at[1]),
        pltpu.make_async_copy(gate_up, w_gu, load_sem.at[2]),
        pltpu.make_async_copy(down, w_dn, load_sem.at[3]),
        pltpu.make_async_copy(down_velocity, v_dn, load_sem.at[4]),
        pltpu.make_async_copy(gate_up_velocity, v_gu, load_sem.at[5]),
    ]
    for load in loads:
        load.start()
    pl.semaphore_wait(barrier, group + 1)

    def z_copy(index, source=None):
        array, chunk = index // CHUNKS, index % CHUNKS
        source = held.at[0, array] if source is None else source
        return pltpu.make_async_remote_copy(
            src_ref=source.at[:, span(chunk)],
            dst_ref=held.at[1, array, :, span(chunk)],
            send_sem=z_send.at[index],
            recv_sem=z_recv.at[index],
            device_id={"expert": opposite},
            device_id_type=MESH,
        )

    info_copy = pltpu.make_async_remote_copy(
        src_ref=info,
        dst_ref=other_info,
        send_sem=z_send.at[2 * CHUNKS],
        recv_sem=z_recv.at[2 * CHUNKS],
        device_id={"expert": opposite},
        device_id_type=MESH,
    )
    info_copy.start()
    for index in range(2 * CHUNKS):
        z_copy(index, (tokens, grads)[index // CHUNKS]).start()

    def choose(part, table):
        names = [table[k : k + 1, :] for k in range(2)]
        weights = [table[2 + k : 3 + k, :] for k in range(2)]
        listed = lax.broadcasted_iota(jnp.int32, (experts, tok_rows), 0).astype(F32)
        member_of = jnp.where((names[0] == listed) | (names[1] == listed), 1.0, 0.0)
        earlier = jnp.where(
            lax.broadcasted_iota(jnp.int32, (tok_rows, tok_rows), 0)
            < lax.broadcasted_iota(jnp.int32, (tok_rows, tok_rows), 1),
            1.0,
            0.0,
        )
        before = matmul(member_of.astype(BF16), earlier.astype(BF16))
        first = (side * part_rows).astype(F32)
        slots = [
            name * float(capacity)
            + jnp.sum(jnp.where(name == listed, before, 0.0), axis=0, keepdims=True)
            - first
            for name in names
        ]
        place = lax.broadcasted_iota(jnp.int32, (part_rows, tok_rows), 0).astype(F32)
        hits = [slot == place for slot in slots]
        picks[0, part] = jnp.where(hits[0] | hits[1], 1.0, 0.0).astype(BF16)
        picks[1, part] = (
            jnp.where(hits[0], weights[0], 0.0) + jnp.where(hits[1], weights[1], 0.0)
        ).astype(BF16)

    def pass_on(source, target, part, chunk, send, recv):
        target[block(part, mine), span(chunk)] = source[block(part, mine), span(chunk)]

        def one(step, carry):
            at = (mine + step) % group
            pltpu.make_async_remote_copy(
                src_ref=source.at[block(part, at), span(chunk)],
                dst_ref=target.at[block(part, mine), span(chunk)],
                send_sem=send,
                recv_sem=recv,
                device_id=member(at),
                device_id_type=MESH,
            ).start()
            return carry

        lax.fori_loop(1, group, one, 0)

    def all_sent_or_here(source, target, cut, send, recv):
        some = pl.ds(0, part_rows - capacity)
        return pltpu.make_async_remote_copy(
            src_ref=source.at[some, cut],
            dst_ref=target.at[some, cut],
            send_sem=send,
            recv_sem=recv,
            device_id={"expert": opposite},
            device_id_type=MESH,
        )

    def half_rows(part, at, count):
        return pl.ds(pl.multiple_of(part * part_rows + at * count, count), count)

    def dispatch(array, part, chunk):
        def one(at, carry):
            slots = pl.ds(pl.multiple_of(at * 128, 128), 128)
            picked = matmul(picks[array, part, slots, :], held[part, array, :, span(chunk)])
            packed[array, half_rows(part, at, 128), span(chunk)] = picked.astype(BF16)
            return carry

        lax.fori_loop(0, part_rows // 128, one, 0)
        pass_on(
            packed.at[array],
            rows.at[array],
            part,
            chunk,
            x_send.at[2 * array + part],
            x_recv.at[(2 * array + part) * CHUNKS + chunk],
        )

    def wait_rows(array, part, chunk):
        all_sent_or_here(
            packed.at[array],
            rows.at[array],
            span(chunk),
            x_send.at[2 * array + part],
            x_recv.at[(2 * array + part) * CHUNKS + chunk],
        ).wait_recv()

    def each(count, step):
        def one(at, carry):
            step(at)
            return carry

        lax.fori_loop(0, count, one, 0)

    def forward(part):
        each(CHUNKS, lambda chunk: wait_rows(0, part, chunk))

        def one(at):
            here = half_rows(part, at, 128)
            pre = matmul(rows[0, here, :], w_gu[...]) * inv_width
            gate = pre[:, :half_width]
            upper = pre[:, half_width:]
            sigmoid = jax.nn.sigmoid(gate)
            active = gate * sigmoid
            hidden[here, :] = (active * upper).astype(BF16)
            factors[here, :half_width] = upper * (sigmoid * (1.0 + gate * (1.0 - sigmoid)))
            factors[here, half_width:] = active
            hidden_grad[here, :] = jnp.zeros((128, half_width), F32)

        each(part_rows // 128, one)

    choose(0, info)
    loads[0].wait()
    loads[1].wait()
    each(2 * CHUNKS, lambda index: dispatch(index // CHUNKS, 0, index % CHUNKS))
    info_copy.wait()
    choose(1, other_info)
    for load in loads[2:]:
        load.wait()

    def take(index):
        copy = z_copy(index)
        copy.wait_recv()
        copy.wait_send()
        dispatch(index // CHUNKS, 1, index % CHUNKS)

    def swap_copy(source, target, at, count, index):
        part = pl.ds(pl.multiple_of(at * count, count), count)
        return pltpu.make_async_remote_copy(
            src_ref=source.at[part],
            dst_ref=target.at[part],
            send_sem=mix_send.at[index],
            recv_sem=mix_recv.at[index],
            device_id={"replica": mate},
            device_id_type=MESH,
        )

    def keep_copy(source, result, index):
        return pltpu.make_async_copy(source, result, store_sem.at[index])

    def stepped(weight, velocity, gradient):
        return (
            weight.astype(F32) - STEP * (DECAY * velocity.astype(F32) + gradient)
        ).astype(BF16)

    def down_chunk(chunk):
        wait_rows(1, 0, chunk)
        wait_rows(1, 1, chunk)

        def term(at):
            those = pl.ds(pl.multiple_of(at * 256, 256), 256)
            hidden_grad[those, :] += matmul(rows[1, those, span(chunk)], w_dn[span(chunk), :])

        each(total // 256, term)

        def update(at):
            here = pl.ds(pl.multiple_of(chunk * columns + at * 256, 256), 256)
            gradient = matmul(rows[1, :, here], hidden[...], 0, 0) * inv_hidden
            new_dn[here, :] = stepped(w_dn[here, :], v_dn[here, :], gradient)

        each(columns // 256, update)
        swap_copy(new_dn, far_dn, chunk, columns, CHUNKS + chunk).start()
        keep_copy(new_dn.at[span(chunk)], out_dn.at[span(chunk)], 0).start()

    def dispatch_step(index):
        @pl.when(index < 2 * CHUNKS)
        def _():
            take(index)

        @pl.when((index == FIRST) | (index == FIRST + FORWARD_GAP))
        def _():
            forward((index - FIRST) // FORWARD_GAP)

        @pl.when(index >= LATE)
        def _():
            down_chunk(index - LATE)

    each(LATE + CHUNKS, dispatch_step)

    def finish(at):
        here = pl.ds(pl.multiple_of(at * 128, 128), 128)
        scaled = hidden_grad[here, :] * inv_hidden
        pre_grad[here, :half_width] = (scaled * factors[here, :half_width]).astype(BF16)
        pre_grad[here, half_width:] = (scaled * factors[here, half_width:]).astype(BF16)

    each(total // 128, finish)

    for part in range(2):
        all_sent_or_here(
            packed.at[0], rows.at[0], slice(None), x_send.at[part], x_recv.at[0]
        ).wait_send()

    def give_back(part, chunk):
        def one(at):
            those = half_rows(part, at, 256)
            pair = matmul(pre_grad[those, :], w_gu[span(chunk), :], 1, 1) * inv_width
            packed[0, those, span(chunk)] = pair.astype(BF16)

        each(part_rows // 256, one)
        pass_on(
            packed.at[0],
            returned,
            part,
            chunk,
            ret_send.at[part],
            ret_recv.at[part * CHUNKS + chunk],
        )

    def gate_up_chunk(chunk):
        def update(at):
            here = pl.ds(pl.multiple_of(chunk * columns + at * 256, 256), 256)
            gradient = matmul(rows[0, :, here], pre_grad[...], 0, 0) * inv_width
            new_gu[here, :] = stepped(w_gu[here, :], v_gu[here, :], gradient)

        each(columns // 256, update)
        swap_copy(new_gu, far_gu, chunk, columns, chunk).start()
        keep_copy(new_gu.at[span(chunk)], out_gu.at[span(chunk)], 1).start()

    def wait_back(part, chunk):
        all_sent_or_here(
            packed.at[0],
            returned,
            span(chunk),
            ret_send.at[part],
            ret_recv.at[part * CHUNKS + chunk],
        ).wait_recv()

    def combine(part, chunk):
        wait_back(part, chunk)
        there = returned[half_rows(part, 0, part_rows), span(chunk)]
        across[part, :, span(chunk)] = matmul(picks[0, part], there, 0, 0).astype(BF16)

    def back_copy(chunk):
        return pltpu.make_async_remote_copy(
            src_ref=across.at[1, :, span(chunk)],
            dst_ref=arrived.at[:, span(chunk)],
            send_sem=back_send.at[chunk],
            recv_sem=back_recv.at[chunk],
            device_id={"expert": opposite},
            device_id_type=MESH,
        )

    def return_step(index):
        @pl.when(index < 2 * CHUNKS)
        def _():
            give_back(1 - index // CHUNKS, index % CHUNKS)

        @pl.when(index < CHUNKS)
        def _():
            gate_up_chunk(index)

        behind = index - LAG

        @pl.when(behind >= 0)
        def _():
            combine(1 - behind // CHUNKS, behind % CHUNKS)

        @pl.when(behind >= CHUNKS)
        def _():
            here = span(behind % CHUNKS)
            keep_copy(across.at[0, :, here], kept.at[:, here], 2).start()

        @pl.when((behind >= 0) & (behind < CHUNKS))
        def _():
            back_copy(behind % CHUNKS).start()

    each(2 * CHUNKS + LAG, return_step)

    def end(copy):
        copy.wait_recv()
        copy.wait_send()

    each(CHUNKS, lambda chunk: end(swap_copy(new_dn, far_dn, chunk, columns, CHUNKS + chunk)))
    each(CHUNKS, lambda chunk: end(swap_copy(new_gu, far_gu, chunk, columns, chunk)))
    each(CHUNKS, lambda chunk: end(back_copy(chunk)))
    keep_copy(new_dn, out_dn, 0).wait()
    keep_copy(new_gu, out_gu, 1).wait()
    keep_copy(across.at[0], kept, 2).wait()
    for part in range(2):
        all_sent_or_here(
            packed.at[1], rows.at[1], slice(None), x_send.at[2 + part], x_recv.at[0]
        ).wait_send()
        all_sent_or_here(
            packed.at[0], returned, slice(None), ret_send.at[part], ret_recv.at[0]
        ).wait_send()


def layer(level, experts, names, shares, *arrays):
    tokens, _, gate_up, down = arrays[:4]
    tok_rows, width = tokens.shape
    twice = gate_up.shape[1]
    single = down.shape[1]
    total = 2 * tok_rows * 2
    part_rows = total // 2
    vmem = pltpu.VMEM
    sems = pltpu.SemaphoreType.DMA
    anywhere = pl.BlockSpec(memory_space=pl.ANY)
    return pl.pallas_call(
        functools.partial(layer_kernel, 1 << level, experts),
        out_shape=(
            jax.ShapeDtypeStruct((width, twice), BF16),
            jax.ShapeDtypeStruct((width, twice), BF16),
            jax.ShapeDtypeStruct((width, single), BF16),
            jax.ShapeDtypeStruct((width, single), BF16),
            jax.ShapeDtypeStruct((tok_rows, width), BF16),
            jax.ShapeDtypeStruct((tok_rows, width), BF16),
        ),
        in_specs=[pl.BlockSpec(memory_space=pltpu.VMEM)] * 2 + [anywhere] * 6,
        out_specs=(anywhere,) * 6,
        scratch_shapes=[
            vmem((8, tok_rows), F32),
            vmem((8, tok_rows), F32),
            vmem((2, 2, tok_rows, width), BF16),
            vmem((2, 2, part_rows, tok_rows), BF16),
            vmem((2, total, width), BF16),
            vmem((2, total, width), BF16),
            vmem((width, twice), BF16),
            vmem((width, single), BF16),
            vmem((width, twice), BF16),
            vmem((width, single), BF16),
            vmem((total, twice), F32),
            vmem((total, single), BF16),
            vmem((total, single), F32),
            vmem((total, twice), BF16),
            vmem((width, twice), BF16),
            vmem((width, single), BF16),
            vmem((total, width), BF16),
            vmem((2, tok_rows, width), BF16),
            sems((6,)),
            sems((3,)),
            sems((2 * CHUNKS + 1,)),
            sems((2 * CHUNKS + 1,)),
            sems((4,)),
            sems((4 * CHUNKS,)),
            sems((2,)),
            sems((2 * CHUNKS,)),
            sems((CHUNKS,)),
            sems((CHUNKS,)),
            sems((2 * CHUNKS,)),
            sems((2 * CHUNKS,)),
        ],
        name=f"layer_shift_{1 << level}",
        compiler_params=pltpu.CompilerParams(
            collective_id=level, has_side_effects=True, vmem_limit_bytes=48 << 20
        ),
    )(names, shares, *arrays)


def per_device(
    tokens,
    out_grad,
    routes,
    route_weight,
    gate_up_matrix,
    down_matrix,
    gate_up_velocity,
    down_velocity,
    partner,
):
    experts = lax.axis_size("expert")
    levels = lax.axis_size("replica").bit_length() - 1
    shift = partner[0]
    level = jnp.zeros((), jnp.int32)
    for bit in range(levels):
        level = level + bit * jnp.bitwise_and(jnp.right_shift(shift, bit), 1)
    own_gu, far_gu, own_dn, far_dn, kept, arrived = lax.switch(
        level,
        [functools.partial(layer, at, experts) for at in range(levels)],
        routes[0].T,
        route_weight[0].T,
        tokens[0],
        out_grad[0],
        gate_up_matrix[0, 0],
        down_matrix[0, 0],
        gate_up_velocity[0, 0],
        down_velocity[0, 0],
    )

    def mean(own, far):
        return (0.5 * (own.astype(F32) + far.astype(F32))).astype(BF16)

    token_grad = (kept.astype(F32) + arrived.astype(F32)).astype(BF16)
    return token_grad[None], mean(own_gu, far_gu)[None, None], mean(own_dn, far_dn)[None, None]


def solution(mesh):
    row = P("replica", "expert", None)
    weight = P("replica", "expert", None, None)
    return jax.shard_map(
        per_device,
        mesh=mesh,
        in_specs=(row,) * 4 + (weight,) * 4 + (P(),),
        out_specs=(row, weight, weight),
        check_vma=False,
    )
```

```python
import functools
import math

import jax
import jax.numpy as jnp
from jax import lax
from jax.experimental import pallas as pl
from jax.experimental.pallas import tpu as pltpu
from jax.sharding import PartitionSpec as P

STEP = 0.2
DECAY = 0.9
MESH = pl.DeviceIdType.MESH
CHUNKS = 8
FIRST = 8
FORWARD_GAP = 2
LATE = 10
LAG = 3
PACE = 1
PACED = (4, 8)
BF16 = jnp.bfloat16
F32 = jnp.float32


def matmul(left, right, left_dim=1, right_dim=0):
    return lax.dot_general(
        left, right, (((left_dim,), (right_dim,)), ((), ())), preferred_element_type=F32
    )


def layer_kernel(
    shift,
    experts,
    names,
    shares,
    tokens,
    grads,
    gate_up,
    down,
    gate_up_velocity,
    down_velocity,
    out_gu,
    far_gu,
    out_dn,
    far_dn,
    kept,
    arrived,
    info,
    other_info,
    held,
    picks,
    packed,
    rows,
    w_gu,
    w_dn,
    v_gu,
    v_dn,
    factors,
    hidden,
    hidden_grad,
    pre_grad,
    new_gu,
    new_dn,
    returned,
    across,
    load_sem,
    store_sem,
    z_send,
    z_recv,
    x_send,
    x_recv,
    ret_send,
    ret_recv,
    back_send,
    back_recv,
    mix_send,
    mix_recv,
):
    tok_rows, width = tokens.shape
    half_width = down.shape[1]
    group = experts // 2
    total = rows.shape[1]
    part_rows = total // 2
    capacity = part_rows // group
    columns = width // CHUNKS
    paced = shift in PACED
    inv_width = 1.0 / math.sqrt(width)
    inv_hidden = 1.0 / math.sqrt(half_width)

    me = lax.axis_index("expert")
    replica = lax.axis_index("replica")
    side = me // group
    mine = me % group
    opposite = (me + group) % experts
    mate = replica + shift - 2 * shift * ((replica // shift) % 2)

    def member(at):
        return {"expert": side * group + at}

    def span(chunk):
        return pl.ds(pl.multiple_of(chunk * columns, columns), columns)

    def block(part, at):
        return pl.ds(pl.multiple_of(part * part_rows + at * capacity, capacity), capacity)

    info[...] = jnp.zeros_like(info)
    info[0:2, :] = names[...].astype(F32)
    info[2:4, :] = shares[...].astype(F32)

    barrier = pltpu.get_barrier_semaphore()
    for step in range(1, group):
        pl.semaphore_signal(
            barrier, inc=1, device_id=member((mine + step) % group), device_id_type=MESH
        )
    pl.semaphore_signal(barrier, inc=1, device_id={"expert": opposite}, device_id_type=MESH)
    pl.semaphore_signal(barrier, inc=1, device_id={"replica": mate}, device_id_type=MESH)

    loads = [
        pltpu.make_async_copy(tokens, held.at[0, 0], load_sem.at[0]),
        pltpu.make_async_copy(grads, held.at[0, 1], load_sem.at[1]),
        pltpu.make_async_copy(gate_up, w_gu, load_sem.at[2]),
        pltpu.make_async_copy(down, w_dn, load_sem.at[3]),
        pltpu.make_async_copy(down_velocity, v_dn, load_sem.at[4]),
        pltpu.make_async_copy(gate_up_velocity, v_gu, load_sem.at[5]),
    ]
    for load in loads:
        load.start()
    pl.semaphore_wait(barrier, group + 1)

    def z_copy(index, source=None):
        array, chunk = index // CHUNKS, index % CHUNKS
        source = held.at[0, array] if source is None else source
        return pltpu.make_async_remote_copy(
            src_ref=source.at[:, span(chunk)],
            dst_ref=held.at[1, array, :, span(chunk)],
            send_sem=z_send.at[index],
            recv_sem=z_recv.at[index],
            device_id={"expert": opposite},
            device_id_type=MESH,
        )

    info_copy = pltpu.make_async_remote_copy(
        src_ref=info,
        dst_ref=other_info,
        send_sem=z_send.at[2 * CHUNKS],
        recv_sem=z_recv.at[2 * CHUNKS],
        device_id={"expert": opposite},
        device_id_type=MESH,
    )
    info_copy.start()
    for index in range(2 * CHUNKS):
        z_copy(index, (tokens, grads)[index // CHUNKS]).start()

    def choose(part, table):
        names = [table[k : k + 1, :] for k in range(2)]
        weights = [table[2 + k : 3 + k, :] for k in range(2)]
        listed = lax.broadcasted_iota(jnp.int32, (experts, tok_rows), 0).astype(F32)
        member_of = jnp.where((names[0] == listed) | (names[1] == listed), 1.0, 0.0)
        earlier = jnp.where(
            lax.broadcasted_iota(jnp.int32, (tok_rows, tok_rows), 0)
            < lax.broadcasted_iota(jnp.int32, (tok_rows, tok_rows), 1),
            1.0,
            0.0,
        )
        before = matmul(member_of.astype(BF16), earlier.astype(BF16))
        first = (side * part_rows).astype(F32)
        slots = [
            name * float(capacity)
            + jnp.sum(jnp.where(name == listed, before, 0.0), axis=0, keepdims=True)
            - first
            for name in names
        ]
        place = lax.broadcasted_iota(jnp.int32, (part_rows, tok_rows), 0).astype(F32)
        hits = [slot == place for slot in slots]
        picks[0, part] = jnp.where(hits[0] | hits[1], 1.0, 0.0).astype(BF16)
        picks[1, part] = (
            jnp.where(hits[0], weights[0], 0.0) + jnp.where(hits[1], weights[1], 0.0)
        ).astype(BF16)

    def pass_on(source, target, part, chunk, send, recv):
        target[block(part, mine), span(chunk)] = source[block(part, mine), span(chunk)]

        def one(step, carry):
            at = (mine + step) % group
            pltpu.make_async_remote_copy(
                src_ref=source.at[block(part, at), span(chunk)],
                dst_ref=target.at[block(part, mine), span(chunk)],
                send_sem=send,
                recv_sem=recv,
                device_id=member(at),
                device_id_type=MESH,
            ).start()
            return carry

        lax.fori_loop(1, group, one, 0)

    def all_sent_or_here(source, target, cut, send, recv):
        some = pl.ds(0, part_rows - capacity)
        return pltpu.make_async_remote_copy(
            src_ref=source.at[some, cut],
            dst_ref=target.at[some, cut],
            send_sem=send,
            recv_sem=recv,
            device_id={"expert": opposite},
            device_id_type=MESH,
        )

    def half_rows(part, at, count):
        return pl.ds(pl.multiple_of(part * part_rows + at * count, count), count)

    def dispatch(array, part, chunk):
        def one(at, carry):
            slots = pl.ds(pl.multiple_of(at * 128, 128), 128)
            picked = matmul(picks[array, part, slots, :], held[part, array, :, span(chunk)])
            packed[array, half_rows(part, at, 128), span(chunk)] = picked.astype(BF16)
            return carry

        lax.fori_loop(0, part_rows // 128, one, 0)
        pass_on(
            packed.at[array],
            rows.at[array],
            part,
            chunk,
            x_send.at[2 * array + part],
            x_recv.at[(2 * array + part) * CHUNKS + chunk],
        )

    def wait_rows(array, part, chunk):
        all_sent_or_here(
            packed.at[array],
            rows.at[array],
            span(chunk),
            x_send.at[2 * array + part],
            x_recv.at[(2 * array + part) * CHUNKS + chunk],
        ).wait_recv()

    def each(count, step):
        def one(at, carry):
            step(at)
            return carry

        lax.fori_loop(0, count, one, 0)

    def forward(part):
        each(CHUNKS, lambda chunk: wait_rows(0, part, chunk))

        def one(at):
            here = half_rows(part, at, 128)
            pre = matmul(rows[0, here, :], w_gu[...]) * inv_width
            gate = pre[:, :half_width]
            upper = pre[:, half_width:]
            sigmoid = jax.nn.sigmoid(gate)
            active = gate * sigmoid
            hidden[here, :] = (active * upper).astype(BF16)
            factors[here, :half_width] = upper * (sigmoid * (1.0 + gate * (1.0 - sigmoid)))
            factors[here, half_width:] = active
            hidden_grad[here, :] = jnp.zeros((128, half_width), F32)

        each(part_rows // 128, one)

    choose(0, info)
    loads[0].wait()
    loads[1].wait()
    each(2 * CHUNKS, lambda index: dispatch(index // CHUNKS, 0, index % CHUNKS))
    info_copy.wait()
    choose(1, other_info)
    for load in loads[2:]:
        load.wait()

    def take(index):
        copy = z_copy(index)
        copy.wait_recv()
        copy.wait_send()
        dispatch(index // CHUNKS, 1, index % CHUNKS)

    def swap_copy(source, target, at, count, index):
        part = pl.ds(pl.multiple_of(at * count, count), count)
        return pltpu.make_async_remote_copy(
            src_ref=source.at[part],
            dst_ref=target.at[part],
            send_sem=mix_send.at[index],
            recv_sem=mix_recv.at[index],
            device_id={"replica": mate},
            device_id_type=MESH,
        )

    def keep_copy(source, result, index):
        return pltpu.make_async_copy(source, result, store_sem.at[index])

    def stepped(weight, velocity, gradient):
        return (
            weight.astype(F32) - STEP * (DECAY * velocity.astype(F32) + gradient)
        ).astype(BF16)

    def down_chunk(chunk):
        wait_rows(1, 0, chunk)
        wait_rows(1, 1, chunk)

        def term(at):
            those = pl.ds(pl.multiple_of(at * 256, 256), 256)
            hidden_grad[those, :] += matmul(rows[1, those, span(chunk)], w_dn[span(chunk), :])

        each(total // 256, term)

        def update(at):
            here = pl.ds(pl.multiple_of(chunk * columns + at * 256, 256), 256)
            gradient = matmul(rows[1, :, here], hidden[...], 0, 0) * inv_hidden
            new_dn[here, :] = stepped(w_dn[here, :], v_dn[here, :], gradient)

        each(columns // 256, update)
        swap_copy(new_dn, far_dn, chunk, columns, CHUNKS + chunk).start()
        keep_copy(new_dn.at[span(chunk)], out_dn.at[span(chunk)], 0).start()

    def dispatch_step(index):
        @pl.when(index < 2 * CHUNKS)
        def _():
            take(index)

        @pl.when((index == FIRST) | (index == FIRST + FORWARD_GAP))
        def _():
            forward((index - FIRST) // FORWARD_GAP)

        @pl.when(index >= LATE)
        def _():
            down_chunk(index - LATE)

    each(LATE + CHUNKS, dispatch_step)

    def finish(at):
        here = pl.ds(pl.multiple_of(at * 128, 128), 128)
        scaled = hidden_grad[here, :] * inv_hidden
        pre_grad[here, :half_width] = (scaled * factors[here, :half_width]).astype(BF16)
        pre_grad[here, half_width:] = (scaled * factors[here, half_width:]).astype(BF16)

    each(total // 128, finish)

    for part in range(2):
        all_sent_or_here(
            packed.at[0], rows.at[0], slice(None), x_send.at[part], x_recv.at[0]
        ).wait_send()

    def give_back(part, chunk):
        def one(at):
            those = half_rows(part, at, 256)
            pair = matmul(pre_grad[those, :], w_gu[span(chunk), :], 1, 1) * inv_width
            packed[0, those, span(chunk)] = pair.astype(BF16)

        each(part_rows // 256, one)
        pass_on(
            packed.at[0],
            returned,
            part,
            chunk,
            ret_send.at[part],
            ret_recv.at[part * CHUNKS + chunk],
        )

    def gate_up_chunk(chunk):
        def update(at):
            here = pl.ds(pl.multiple_of(chunk * columns + at * 256, 256), 256)
            gradient = matmul(rows[0, :, here], pre_grad[...], 0, 0) * inv_width
            new_gu[here, :] = stepped(w_gu[here, :], v_gu[here, :], gradient)

        each(columns // 256, update)
        if not paced:
            swap_copy(new_gu, far_gu, chunk, columns, chunk).start()
        keep_copy(new_gu.at[span(chunk)], out_gu.at[span(chunk)], 1).start()

    def wait_back(part, chunk):
        all_sent_or_here(
            packed.at[0],
            returned,
            span(chunk),
            ret_send.at[part],
            ret_recv.at[part * CHUNKS + chunk],
        ).wait_recv()

    def combine(part, chunk):
        wait_back(part, chunk)
        there = returned[half_rows(part, 0, part_rows), span(chunk)]
        across[part, :, span(chunk)] = matmul(picks[0, part], there, 0, 0).astype(BF16)

    def back_copy(chunk):
        return pltpu.make_async_remote_copy(
            src_ref=across.at[1, :, span(chunk)],
            dst_ref=arrived.at[:, span(chunk)],
            send_sem=back_send.at[chunk],
            recv_sem=back_recv.at[chunk],
            device_id={"expert": opposite},
            device_id_type=MESH,
        )

    def return_step(index):
        @pl.when(index < 2 * CHUNKS)
        def _():
            give_back(1 - index // CHUNKS, index % CHUNKS)

        @pl.when(index < CHUNKS)
        def _():
            gate_up_chunk(index)

        behind = index - LAG

        @pl.when(behind >= 0)
        def _():
            combine(1 - behind // CHUNKS, behind % CHUNKS)

        @pl.when(behind >= CHUNKS)
        def _():
            here = span(behind % CHUNKS)
            keep_copy(across.at[0, :, here], kept.at[:, here], 2).start()

        @pl.when((behind >= 0) & (behind < CHUNKS))
        def _():
            back_copy(behind % CHUNKS).start()
            if paced:

                @pl.when(behind >= PACE)
                def _():
                    back_copy(behind - PACE).wait_send()

                swap_copy(new_gu, far_gu, behind % CHUNKS, columns, behind % CHUNKS).start()

    each(2 * CHUNKS + LAG, return_step)

    def end(copy):
        copy.wait_recv()
        copy.wait_send()

    each(CHUNKS, lambda chunk: end(swap_copy(new_dn, far_dn, chunk, columns, CHUNKS + chunk)))
    each(CHUNKS, lambda chunk: end(swap_copy(new_gu, far_gu, chunk, columns, chunk)))
    each(CHUNKS, lambda chunk: back_copy(chunk).wait_recv())
    sent = CHUNKS - PACE if paced else 0
    each(CHUNKS - sent, lambda chunk: back_copy(sent + chunk).wait_send())
    keep_copy(new_dn, out_dn, 0).wait()
    keep_copy(new_gu, out_gu, 1).wait()
    keep_copy(across.at[0], kept, 2).wait()
    for part in range(2):
        all_sent_or_here(
            packed.at[1], rows.at[1], slice(None), x_send.at[2 + part], x_recv.at[0]
        ).wait_send()
        all_sent_or_here(
            packed.at[0], returned, slice(None), ret_send.at[part], ret_recv.at[0]
        ).wait_send()


def layer(level, experts, names, shares, *arrays):
    tokens, _, gate_up, down = arrays[:4]
    tok_rows, width = tokens.shape
    twice = gate_up.shape[1]
    single = down.shape[1]
    total = 2 * tok_rows * 2
    part_rows = total // 2
    vmem = pltpu.VMEM
    sems = pltpu.SemaphoreType.DMA
    anywhere = pl.BlockSpec(memory_space=pl.ANY)
    return pl.pallas_call(
        functools.partial(layer_kernel, 1 << level, experts),
        out_shape=(
            jax.ShapeDtypeStruct((width, twice), BF16),
            jax.ShapeDtypeStruct((width, twice), BF16),
            jax.ShapeDtypeStruct((width, single), BF16),
            jax.ShapeDtypeStruct((width, single), BF16),
            jax.ShapeDtypeStruct((tok_rows, width), BF16),
            jax.ShapeDtypeStruct((tok_rows, width), BF16),
        ),
        in_specs=[pl.BlockSpec(memory_space=pltpu.VMEM)] * 2 + [anywhere] * 6,
        out_specs=(anywhere,) * 6,
        scratch_shapes=[
            vmem((8, tok_rows), F32),
            vmem((8, tok_rows), F32),
            vmem((2, 2, tok_rows, width), BF16),
            vmem((2, 2, part_rows, tok_rows), BF16),
            vmem((2, total, width), BF16),
            vmem((2, total, width), BF16),
            vmem((width, twice), BF16),
            vmem((width, single), BF16),
            vmem((width, twice), BF16),
            vmem((width, single), BF16),
            vmem((total, twice), F32),
            vmem((total, single), BF16),
            vmem((total, single), F32),
            vmem((total, twice), BF16),
            vmem((width, twice), BF16),
            vmem((width, single), BF16),
            vmem((total, width), BF16),
            vmem((2, tok_rows, width), BF16),
            sems((6,)),
            sems((3,)),
            sems((2 * CHUNKS + 1,)),
            sems((2 * CHUNKS + 1,)),
            sems((4,)),
            sems((4 * CHUNKS,)),
            sems((2,)),
            sems((2 * CHUNKS,)),
            sems((CHUNKS,)),
            sems((CHUNKS,)),
            sems((2 * CHUNKS,)),
            sems((2 * CHUNKS,)),
        ],
        name=f"layer_shift_{1 << level}",
        compiler_params=pltpu.CompilerParams(
            collective_id=level, has_side_effects=True, vmem_limit_bytes=48 << 20
        ),
    )(names, shares, *arrays)


def per_device(
    tokens,
    out_grad,
    routes,
    route_weight,
    gate_up_matrix,
    down_matrix,
    gate_up_velocity,
    down_velocity,
    partner,
):
    experts = lax.axis_size("expert")
    levels = lax.axis_size("replica").bit_length() - 1
    shift = partner[0]
    level = jnp.zeros((), jnp.int32)
    for bit in range(levels):
        level = level + bit * jnp.bitwise_and(jnp.right_shift(shift, bit), 1)
    own_gu, far_gu, own_dn, far_dn, kept, arrived = lax.switch(
        level,
        [functools.partial(layer, at, experts) for at in range(levels)],
        routes[0].T,
        route_weight[0].T,
        tokens[0],
        out_grad[0],
        gate_up_matrix[0, 0],
        down_matrix[0, 0],
        gate_up_velocity[0, 0],
        down_velocity[0, 0],
    )

    def mean(own, far):
        return (0.5 * (own.astype(F32) + far.astype(F32))).astype(BF16)

    token_grad = (kept.astype(F32) + arrived.astype(F32)).astype(BF16)
    return token_grad[None], mean(own_gu, far_gu)[None, None], mean(own_dn, far_dn)[None, None]


def solution(mesh):
    row = P("replica", "expert", None)
    weight = P("replica", "expert", None, None)
    return jax.shard_map(
        per_device,
        mesh=mesh,
        in_specs=(row,) * 4 + (weight,) * 4 + (P(),),
        out_specs=(row, weight, weight),
        check_vma=False,
    )
```
